32 devices in a mesh: pair: 2 (over core), vcol: 16 (over z, y, x).
Axes of the slice: x: 2, y: 2, z: 4, core: 2. Of those that a mesh axis runs over, the one named last changes fastest.
Arguments:
- amplitudes: bfloat16 [1280, 4096], P('pair', 'vcol'), may hold values from -6 to 6
- tile_owner: int32 [32], replicated, may hold values from 0 to 31, each once
- integrals: bfloat16 [4096, 4096], P('pair', 'vcol'), may hold values from -0.125 to 0.125
- screening: int32 [20, 32, 32], P('pair'), may hold values 0 or 1
- occ_energy: float32 [1280], P('pair'), may hold values from -1 to -0.2
- virt_energy: float32 [4096], replicated, may hold values from 0.2 to 1
Outputs:
- residual: bfloat16 [1280, 4096], P('pair', 'vcol')
The draws below stay inside these ranges and needn't reach their ends.
Inputs may be any that keep to these rules, and one draw needn't show every extreme that they name: `tile_owner`: each of the 32 tiles appears exactly once.
All inputs are finite; a program needn't handle non-finite values. No bound on the sum of `screening` on one device may be relied on, other than what follows from the above.
Results may differ from the reference program's by a relative error of at most 0.0036.
Values may be sent and summed in bfloat16 or wider, within the bound.
A program may use at most 64 MiB of HBM per device.

```python
import jax
import jax.numpy as jnp
from jax import lax

TILE = 128
PBLK = 64
PAIRS = 1280
KT = 32
K = 4096
NPB = 20


def plant(result, own_key, low, high):
    dims = result.shape
    index_at = [jax.random.randint(jax.random.fold_in(own_key, axis), (), 0, dims[axis]) for axis in range(len(dims))]
    result = result.at[tuple(index_at)].set(low)
    longest = dims.index(max(dims))
    index_at[longest] = (index_at[longest] + 1) % dims[longest]
    return result.at[tuple(index_at)].set(high)


def strengthened(result, own_key, source, target, shards_of, factor):
    owner, partner = [(jnp.arange(result.shape[dim]) // (result.shape[dim] // shards_of)).reshape([-1 if axis == dim else 1 for axis in range(result.ndim)]) for dim in (source, target)]
    chosen = jax.random.permutation(own_key, shards_of)[partner]
    strong = (owner == chosen) | (owner == (partner + shards_of // 2) % shards_of)
    return jnp.where(strong, factor * result, result)


def block_scale(rng, extent, pieces, smallest, top_value):
    loudness, own = 1.0, jax.random.fold_in(rng, 6)
    for dim, shards_of in pieces:
        draws = jnp.exp(jax.random.uniform(jax.random.fold_in(own, dim), (shards_of,), jnp.float32, smallest / len(pieces), top_value / len(pieces)))
        loudness = loudness * jnp.repeat(draws, extent[dim] // shards_of).reshape([-1 if axis == dim else 1 for axis in range(len(extent))])
    return loudness


def noise(stream_key, shape, scale, limit, cuts=(), kind=jnp.bfloat16):
    array = scale * jax.random.normal(stream_key, shape, jnp.float32)
    if cuts:
        array = array * block_scale(stream_key, shape, cuts, -0.22, 0.18)
    return jnp.clip(array, -limit, limit).astype(kind)


def heavy_noise(own_key, shape, deviation, reach, split, heavy, held_as=jnp.bfloat16):
    values = deviation * jax.random.normal(own_key, shape, jnp.float32)
    if split:
        values = values * block_scale(own_key, shape, split, -0.22, 0.18)
    return jnp.clip(strengthened(values, jax.random.fold_in(own_key, 3), *heavy), -reach, reach).astype(held_as)


def setup_inputs(seed: int = 0) -> dict:
    arg_keys = jax.random.split(jax.random.key(seed), 7)
    amplitudes = noise(arg_keys[0], (PAIRS, K), 1.0, 6.0, ((0, 2), (1, 16)))
    tile_owner = jax.random.permutation(arg_keys[1], KT).astype(jnp.int32)
    integrals = heavy_noise(arg_keys[2], (K, K), K ** -0.5, 0.125, ((0, 2), (1, 16)), (0, 1, 16, 2.0))
    screening = plant((jax.random.randint(arg_keys[3], (NPB, KT, KT), 0, 4) < 3).astype(jnp.int32), jax.random.fold_in(arg_keys[3], 1), 0, 1)
    occ_energy = jnp.clip(-1.0 + 0.8 * jax.random.uniform(arg_keys[4], (PAIRS,), jnp.float32) ** block_scale(arg_keys[4], (PAIRS,), ((0, 2),), -0.2, 0.2), -1.0, -0.2)
    virt_energy = jnp.clip(jax.random.uniform(arg_keys[5], (K,), jnp.float32, 0.2, 1.0), 0.2, 1.0)
    return {"amplitudes": amplitudes, "tile_owner": tile_owner, "integrals": integrals, "screening": screening, "occ_energy": occ_energy, "virt_energy": virt_energy}


def reference(amplitudes, tile_owner, integrals, screening, occ_energy, virt_energy):
    pair_count = amplitudes.shape[0]
    tile_count = tile_owner.shape[0]
    slot_tiles = amplitudes.reshape(pair_count, tile_count, TILE)
    natural = jnp.zeros_like(slot_tiles).at[:, tile_owner].set(slot_tiles).reshape(pair_count, tile_count * TILE)
    grid_ints = integrals.reshape(tile_count, TILE, tile_count, TILE)
    blocks = natural.reshape(pair_count // PBLK, PBLK, tile_count * TILE)

    def one_block(operands):
        left_rows, marks = operands
        masked = (grid_ints * marks.astype(grid_ints.dtype)[:, None, :, None]).reshape(tile_count * TILE, tile_count * TILE)
        return jnp.dot(left_rows, masked, preferred_element_type=jnp.float32)

    ladder = lax.map(one_block, (blocks, screening)).reshape(pair_count, tile_count * TILE).astype(jnp.bfloat16)
    owned_tiles = ladder.reshape(pair_count, tile_count, TILE)[:, tile_owner].reshape(pair_count, tile_count * TILE).astype(jnp.float32)
    virt_owned = virt_energy.reshape(tile_count, TILE)[tile_owner].reshape(tile_count * TILE)
    residual = owned_tiles + (virt_owned[None, :] - occ_energy[:, None]) * amplitudes.astype(jnp.float32)
    return residual.astype(jnp.bfloat16)
```

```python
import jax
import jax.numpy as jnp
from jax import lax
from jax.sharding import PartitionSpec as P

TILE = 128
PBLK = 64
KT_DEV = 2


def one_hot(indices, length):
    return (indices[:, None] == jnp.arange(length, dtype=jnp.int32)[None, :]).astype(jnp.float32)


def gather_rows(panel):
    return lax.all_gather(panel, "pair", axis=0, tiled=True)


def local(amplitudes, tile_owner, integrals, screening, occ_energy, virt_energy):
    pair_local = amplitudes.shape[0]
    tile_count = tile_owner.shape[0]
    width = KT_DEV * TILE
    block_count = pair_local // PBLK
    column = lax.axis_index("vcol")
    first_slot = column * KT_DEV
    owned_tiles = lax.dynamic_slice_in_dim(tile_owner, first_slot, KT_DEV, 0)
    screen_float = screening.astype(jnp.float32)
    natural_tiles = first_slot + jnp.arange(KT_DEV, dtype=jnp.int32)
    panel = gather_rows(integrals)
    picked = jnp.einsum("bct,jt->bcj", screen_float, one_hot(natural_tiles, tile_count))
    marks_slot = jnp.take(picked, tile_owner, axis=1).astype(jnp.bfloat16)
    panel_slot = jnp.take(panel.reshape(tile_count, TILE, width), tile_owner, axis=0)
    piece_in = lax.all_gather(amplitudes, "vcol", axis=1, tiled=True)
    tiles_in = piece_in.shape[1] // TILE
    left_all = piece_in.reshape(block_count, PBLK, tiles_in * TILE)

    def one_block(operands):
        left_rows, marks = operands
        masked = (
            panel_slot.reshape(tiles_in, TILE, KT_DEV, TILE) * marks[:, None, :, None]
        ).reshape(tiles_in * TILE, width)
        return jnp.dot(left_rows, masked, preferred_element_type=jnp.float32)

    summed = lax.map(one_block, (left_all, marks_slot))
    ladder_local = summed.reshape(pair_local, width).astype(jnp.bfloat16)
    ranks = tile_count // KT_DEV
    rows = pair_local // ranks
    parts = ladder_local.reshape(ranks, rows, KT_DEV, TILE).transpose(0, 2, 1, 3)
    spread = lax.all_to_all(parts, "vcol", 0, 0, tiled=True).reshape(tile_count, rows, TILE)
    by_slot = jnp.take(spread, tile_owner, axis=0).reshape(ranks, KT_DEV, rows, TILE)
    back = lax.all_to_all(by_slot, "vcol", 0, 0, tiled=True)
    ladder_owned = back.transpose(0, 2, 1, 3).reshape(pair_local, width).astype(jnp.float32)
    virt_owned = jnp.dot(
        one_hot(owned_tiles, tile_count),
        virt_energy.reshape(tile_count, TILE),
        precision=lax.Precision.HIGHEST,
    ).reshape(width)
    residual = ladder_owned + (virt_owned[None, :] - occ_energy[:, None]) * amplitudes.astype(
        jnp.float32
    )
    return residual.astype(jnp.bfloat16)


def solution(mesh):
    return jax.shard_map(
        local,
        mesh=mesh,
        in_specs=(P("pair", "vcol"), P(), P("pair", "vcol"), P("pair", None, None), P("pair"), P()),
        out_specs=P("pair", "vcol"),
        check_vma=False,
    )
```

```python
import functools

import jax
import jax.numpy as jnp
from jax import lax
from jax.experimental import pallas as pl
from jax.experimental.pallas import tpu as pltpu
from jax.sharding import PartitionSpec as P

TILE = 128
PBLK = 64
KT_DEV = 2
MESH = pl.DeviceIdType.MESH


def one_hot(indices, length):
    return (indices[:, None] == jnp.arange(length, dtype=jnp.int32)[None, :]).astype(jnp.float32)


def ladder_kernel(
    ranks, pairs, owner, screen, amps, ints, out,
    gath, panel, lhs, acc,
    local_sem, send_sem, recv_sem, pair_send, pair_recv,
):
    length = ranks // 4
    me = lax.axis_index("vcol")
    core = lax.axis_index("pair")
    line, spot = me // 4, me % 4
    hi, lo = spot // 2, spot % 2
    turn = core % 2
    flip_lo, flip_hi = hi * 2 + 1 - lo, (1 - hi) * 2 + lo
    first = (1 - turn) * flip_lo + turn * flip_hi
    second = turn * flip_lo + (1 - turn) * flip_hi
    across = 3 - spot
    rows = gath.shape[1]
    blocks = rows // PBLK
    tiles = ints.shape[0]

    own_amps = pltpu.make_async_copy(amps, gath.at[me], local_sem.at[0])
    own_ints = pltpu.make_async_copy(ints, panel.at[pl.ds(core * tiles, tiles)], local_sem.at[1])
    own_amps.start()
    own_ints.start()

    has_up, has_down = line < length - 1, line > 0
    first_rank, second_rank = line * 4 + first, line * 4 + second
    barrier = pltpu.get_barrier_semaphore()

    def greet(target):
        pl.semaphore_signal(barrier, inc=1, device_id={"vcol": target}, device_id_type=MESH)

    greet(first_rank)
    greet(second_rank)
    for step in range(1, pairs):
        pl.semaphore_signal(
            barrier, inc=1, device_id={"pair": (core + step) % pairs}, device_id_type=MESH
        )

    @pl.when(has_up)
    def _():
        greet(me + 4)

    @pl.when(has_down)
    def _():
        greet(me - 4)

    pl.semaphore_wait(
        barrier, 1 + pairs + has_up.astype(jnp.int32) + has_down.astype(jnp.int32)
    )

    def shard(source, way, target):
        return pltpu.make_async_remote_copy(
            src_ref=gath.at[source], dst_ref=gath.at[source],
            send_sem=send_sem.at[way, source], recv_sem=recv_sem.at[source],
            device_id={"vcol": target}, device_id_type=MESH,
        )

    def panel_copy(step):
        return pltpu.make_async_remote_copy(
            src_ref=ints, dst_ref=panel.at[pl.ds(core * tiles, tiles)],
            send_sem=pair_send.at[step - 1], recv_sem=pair_recv.at[step - 1],
            device_id={"pair": (core + step) % pairs}, device_id_type=MESH,
        )

    def arrived(source):
        shard(source, 3, second_rank).wait_recv()

    def multiply(source):
        t0, t1 = owner[KT_DEV * source], owner[KT_DEV * source + 1]
        for slot, tile in enumerate((t0, t1)):
            columns = slice(slot * TILE, (slot + 1) * TILE)
            for block in range(blocks):
                part = slice(block * PBLK, (block + 1) * PBLK)
                value = gath[source, part, columns]
                for n in range(KT_DEV):
                    mark = screen[block, tile, KT_DEV * me + n].astype(jnp.float32)
                    lhs[n, part, columns] = value * jnp.full(value.shape, mark, jnp.float32).astype(
                        value.dtype
                    )
        right = jnp.concatenate([panel[t0], panel[t1]], axis=0)
        for n in range(KT_DEV):
            columns = slice(n * TILE, (n + 1) * TILE)
            acc[:, columns] += jnp.dot(
                lhs[n], right[:, columns], preferred_element_type=jnp.float32
            )

    def offset(e):
        return ((e + 1) // 2) * (1 - 2 * (e % 2))

    def inside(e):
        at = line + offset(e)
        return (at >= 0) & (at < length)

    own_amps.wait()

    @pl.when(has_up)
    def _():
        shard(me, 0, me + 4).start()

    @pl.when(has_down)
    def _():
        shard(me, 1, me - 4).start()

    shard(me, 2, first_rank).start()
    shard(me, 3, second_rank).start()
    for step in range(1, pairs):
        panel_copy(step).start()
    acc[...] = jnp.zeros_like(acc)
    own_ints.wait()
    for step in range(1, pairs):
        panel_copy(step).wait_recv()
    multiply(me)

    last = 2 * length - 1

    def on_column(e, _):
        source = (line + offset(e)) * 4 + spot

        @pl.when((e < last) & inside(e))
        def _():
            arrived(source)

            @pl.when((e % 2 == 1) & has_up)
            def _():
                shard(source, 0, me + 4).start()

            @pl.when((e % 2 == 0) & has_down)
            def _():
                shard(source, 1, me - 4).start()

            shard(source, 2, first_rank).start()
            shard(source, 3, second_rank).start()
            multiply(source)

        late = e - 2
        beside = (line + offset(late)) * 4 + first

        @pl.when((late >= 0) & inside(late))
        def _():
            arrived(beside)
            shard(beside, 3, second_rank).start()
            multiply(beside)

        return 0

    lax.fori_loop(1, last + 2, on_column, 0)

    def far_side(e, _):
        @pl.when((e < last) & inside(e))
        def _():
            source = (line + offset(e)) * 4 + second
            arrived(source)
            multiply(source)

        late = e - 2

        @pl.when((late >= 0) & inside(late))
        def _():
            source = (line + offset(late)) * 4 + across
            arrived(source)
            multiply(source)

        return 0

    lax.fori_loop(0, last + 2, far_side, 0)

    part = rows // ranks
    for i in range(ranks):
        for n in range(KT_DEV):
            out[i, n] = acc[i * part : (i + 1) * part, n * TILE : (n + 1) * TILE].astype(out.dtype)

    def drain(e, _):
        @pl.when(inside(e))
        def _():
            source = (line + offset(e)) * 4 + spot

            @pl.when(((e % 2 == 1) | (e == 0)) & has_up)
            def _():
                shard(source, 0, me + 4).wait_send()

            @pl.when((e % 2 == 0) & has_down)
            def _():
                shard(source, 1, me - 4).wait_send()

            shard(source, 2, first_rank).wait_send()
            shard(source, 3, second_rank).wait_send()
            shard((line + offset(e)) * 4 + first, 3, second_rank).wait_send()

        return 0

    lax.fori_loop(0, last, drain, 0)
    for step in range(1, pairs):
        panel_copy(step).wait_send()


def ladder(ranks, pairs, amplitudes, tile_owner, integrals, screening):
    rows, width = amplitudes.shape
    tiles = integrals.shape[0] // TILE
    vmem, smem = pl.BlockSpec(memory_space=pltpu.VMEM), pl.BlockSpec(memory_space=pltpu.SMEM)
    return pl.pallas_call(
        functools.partial(ladder_kernel, ranks, pairs),
        out_shape=jax.ShapeDtypeStruct((ranks, KT_DEV, rows // ranks, TILE), jnp.bfloat16),
        in_specs=[smem, smem, vmem, vmem],
        out_specs=vmem,
        scratch_shapes=[
            pltpu.VMEM((ranks, rows, width), jnp.bfloat16),
            pltpu.VMEM((tiles * pairs, TILE, width), jnp.bfloat16),
            pltpu.VMEM((KT_DEV, rows, width), jnp.bfloat16),
            pltpu.VMEM((rows, width), jnp.float32),
            pltpu.SemaphoreType.DMA((2,)),
            pltpu.SemaphoreType.DMA((4, ranks)),
            pltpu.SemaphoreType.DMA((ranks,)),
            pltpu.SemaphoreType.DMA((pairs - 1,)),
            pltpu.SemaphoreType.DMA((pairs - 1,)),
        ],
        compiler_params=pltpu.CompilerParams(
            collective_id=0, has_side_effects=True, vmem_limit_bytes=48 * 1024 * 1024
        ),
    )(tile_owner, screening, amplitudes, integrals.reshape(tiles, TILE, width))


def local(ranks, pairs, amplitudes, tile_owner, integrals, screening, occ_energy, virt_energy):
    pair_local = amplitudes.shape[0]
    tile_count = tile_owner.shape[0]
    width = KT_DEV * TILE
    column = lax.axis_index("vcol")
    owned_tiles = lax.dynamic_slice_in_dim(tile_owner, column * KT_DEV, KT_DEV, 0)
    rows = pair_local // ranks
    parts = ladder(ranks, pairs, amplitudes, tile_owner, integrals, screening)
    spread = lax.all_to_all(parts, "vcol", 0, 0, tiled=True).reshape(tile_count, rows, TILE)
    by_slot = jnp.take(spread, tile_owner, axis=0).reshape(ranks, KT_DEV, rows, TILE)
    back = lax.all_to_all(by_slot, "vcol", 0, 0, tiled=True)
    ladder_owned = back.transpose(0, 2, 1, 3).reshape(pair_local, width).astype(jnp.float32)
    virt_owned = jnp.dot(
        one_hot(owned_tiles, tile_count),
        virt_energy.reshape(tile_count, TILE),
        precision=lax.Precision.HIGHEST,
    ).reshape(width)
    residual = ladder_owned + (virt_owned[None, :] - occ_energy[:, None]) * amplitudes.astype(
        jnp.float32
    )
    return residual.astype(jnp.bfloat16)


def solution(mesh):
    return jax.shard_map(
        functools.partial(local, mesh.shape["vcol"], mesh.shape["pair"]),
        mesh=mesh,
        in_specs=(P("pair", "vcol"), P(), P("pair", "vcol"), P("pair", None, None), P("pair"), P()),
        out_specs=P("pair", "vcol"),
        check_vma=False,
    )
```

```python
import functools

import jax
import jax.numpy as jnp
from jax import lax
from jax.experimental import pallas as pl
from jax.experimental.pallas import tpu as pltpu
from jax.sharding import PartitionSpec as P

TILE = 128
PBLK = 64
KT_DEV = 2
MESH = pl.DeviceIdType.MESH


def one_hot(indices, length):
    return (indices[:, None] == jnp.arange(length, dtype=jnp.int32)[None, :]).astype(jnp.float32)


def ladder_kernel(
    ranks, pairs, owner, screen, amps, ints, out,
    gath, panel, lhs, acc, parts, natural, slots, landed,
    local_sem, send_sem, recv_sem, pair_send, pair_recv, out_send, out_recv, back_send, back_recv,
):
    length = ranks // 4
    me = lax.axis_index("vcol")
    core = lax.axis_index("pair")
    line, spot = me // 4, me % 4
    hi, lo = spot // 2, spot % 2
    turn = core % 2
    flip_lo, flip_hi = hi * 2 + 1 - lo, (1 - hi) * 2 + lo
    first = (1 - turn) * flip_lo + turn * flip_hi
    second = turn * flip_lo + (1 - turn) * flip_hi
    across = 3 - spot
    rows = gath.shape[1]
    blocks = rows // PBLK
    tiles = ints.shape[0]

    own_amps = pltpu.make_async_copy(amps, gath.at[me], local_sem.at[0])
    own_ints = pltpu.make_async_copy(ints, panel.at[pl.ds(core * tiles, tiles)], local_sem.at[1])
    own_amps.start()
    own_ints.start()

    has_up, has_down = line < length - 1, line > 0
    first_rank, second_rank = line * 4 + first, line * 4 + second
    barrier = pltpu.get_barrier_semaphore()

    def greet(target):
        pl.semaphore_signal(barrier, inc=1, device_id={"vcol": target}, device_id_type=MESH)

    def greet_step(step, _):
        greet((me + step) % ranks)
        return 0

    lax.fori_loop(1, ranks, greet_step, 0)
    for step in range(1, pairs):
        pl.semaphore_signal(
            barrier, inc=1, device_id={"pair": (core + step) % pairs}, device_id_type=MESH
        )

    pl.semaphore_wait(barrier, ranks - 1 + pairs - 1)

    def shard(source, way, target):
        return pltpu.make_async_remote_copy(
            src_ref=gath.at[source], dst_ref=gath.at[source],
            send_sem=send_sem.at[way, source], recv_sem=recv_sem.at[source],
            device_id={"vcol": target}, device_id_type=MESH,
        )

    def panel_copy(step):
        return pltpu.make_async_remote_copy(
            src_ref=ints, dst_ref=panel.at[pl.ds(core * tiles, tiles)],
            send_sem=pair_send.at[step - 1], recv_sem=pair_recv.at[step - 1],
            device_id={"pair": (core + step) % pairs}, device_id_type=MESH,
        )

    def arrived(source):
        shard(source, 3, second_rank).wait_recv()

    def multiply(source):
        t0, t1 = owner[KT_DEV * source], owner[KT_DEV * source + 1]
        for slot, tile in enumerate((t0, t1)):
            columns = slice(slot * TILE, (slot + 1) * TILE)
            for block in range(blocks):
                part = slice(block * PBLK, (block + 1) * PBLK)
                value = gath[source, part, columns]
                for n in range(KT_DEV):
                    mark = screen[block, tile, KT_DEV * me + n].astype(jnp.float32)
                    lhs[n, part, columns] = value * jnp.full(value.shape, mark, jnp.float32).astype(
                        value.dtype
                    )
        right = jnp.concatenate([panel[t0], panel[t1]], axis=0)
        for n in range(KT_DEV):
            columns = slice(n * TILE, (n + 1) * TILE)
            acc[:, columns] += jnp.dot(
                lhs[n], right[:, columns], preferred_element_type=jnp.float32
            )

    def offset(e):
        return ((e + 1) // 2) * (1 - 2 * (e % 2))

    def inside(e):
        at = line + offset(e)
        return (at >= 0) & (at < length)

    own_amps.wait()

    @pl.when(has_up)
    def _():
        shard(me, 0, me + 4).start()

    @pl.when(has_down)
    def _():
        shard(me, 1, me - 4).start()

    shard(me, 2, first_rank).start()
    shard(me, 3, second_rank).start()
    for step in range(1, pairs):
        panel_copy(step).start()
    acc[...] = jnp.zeros_like(acc)
    own_ints.wait()
    for step in range(1, pairs):
        panel_copy(step).wait_recv()
    multiply(me)

    last = 2 * length - 1

    def on_column(e, _):
        source = (line + offset(e)) * 4 + spot

        @pl.when((e < last) & inside(e))
        def _():
            arrived(source)

            @pl.when((e % 2 == 1) & has_up)
            def _():
                shard(source, 0, me + 4).start()

            @pl.when((e % 2 == 0) & has_down)
            def _():
                shard(source, 1, me - 4).start()

            shard(source, 2, first_rank).start()
            shard(source, 3, second_rank).start()
            multiply(source)

        late = e - 2
        beside = (line + offset(late)) * 4 + first

        @pl.when((late >= 0) & inside(late))
        def _():
            arrived(beside)
            shard(beside, 3, second_rank).start()
            multiply(beside)

        return 0

    lax.fori_loop(1, last + 2, on_column, 0)

    def far_side(e, _):
        @pl.when((e < last) & inside(e))
        def _():
            source = (line + offset(e)) * 4 + second
            arrived(source)
            multiply(source)

        late = e - 2

        @pl.when((late >= 0) & inside(late))
        def _():
            source = (line + offset(late)) * 4 + across
            arrived(source)
            multiply(source)

        return 0

    lax.fori_loop(0, last + 2, far_side, 0)

    part = rows // ranks
    for i in range(ranks):
        for n in range(KT_DEV):
            parts[i, n] = acc[i * part : (i + 1) * part, n * TILE : (n + 1) * TILE].astype(
                parts.dtype
            )

    def out_copy(step):
        target = (me + step) % ranks
        return pltpu.make_async_remote_copy(
            src_ref=parts.at[target], dst_ref=natural.at[pl.ds(KT_DEV * me, KT_DEV)],
            send_sem=out_send.at[step - 1], recv_sem=out_recv.at[step - 1],
            device_id={"vcol": target}, device_id_type=MESH,
        )

    def back_copy(step):
        target = (me + step) % ranks
        return pltpu.make_async_remote_copy(
            src_ref=slots.at[pl.ds(KT_DEV * target, KT_DEV)], dst_ref=landed.at[me],
            send_sem=back_send.at[step - 1], recv_sem=back_recv.at[step - 1],
            device_id={"vcol": target}, device_id_type=MESH,
        )

    def each_peer(action):
        def body(step, _):
            action(step)
            return 0

        lax.fori_loop(1, ranks, body, 0)

    own_out = pltpu.make_async_copy(
        parts.at[me], natural.at[pl.ds(KT_DEV * me, KT_DEV)], local_sem.at[2]
    )
    own_back = pltpu.make_async_copy(
        slots.at[pl.ds(KT_DEV * me, KT_DEV)], landed.at[me], local_sem.at[3]
    )
    each_peer(lambda step: out_copy(step).start())
    own_out.start()
    own_out.wait()
    each_peer(lambda step: out_copy(step).wait_recv())
    for slot in range(KT_DEV * ranks):
        slots[slot] = natural[owner[slot]]
    each_peer(lambda step: back_copy(step).start())
    own_back.start()
    own_back.wait()

    def drain(e, _):
        @pl.when(inside(e))
        def _():
            source = (line + offset(e)) * 4 + spot

            @pl.when(((e % 2 == 1) | (e == 0)) & has_up)
            def _():
                shard(source, 0, me + 4).wait_send()

            @pl.when((e % 2 == 0) & has_down)
            def _():
                shard(source, 1, me - 4).wait_send()

            shard(source, 2, first_rank).wait_send()
            shard(source, 3, second_rank).wait_send()
            shard((line + offset(e)) * 4 + first, 3, second_rank).wait_send()

        return 0

    lax.fori_loop(0, last, drain, 0)
    for step in range(1, pairs):
        panel_copy(step).wait_send()
    each_peer(lambda step: out_copy(step).wait_send())
    each_peer(lambda step: back_copy(step).wait_recv())
    out[...] = landed[...]
    each_peer(lambda step: back_copy(step).wait_send())


def ladder(ranks, pairs, amplitudes, tile_owner, integrals, screening):
    rows, width = amplitudes.shape
    tiles = integrals.shape[0] // TILE
    vmem, smem = pl.BlockSpec(memory_space=pltpu.VMEM), pl.BlockSpec(memory_space=pltpu.SMEM)
    hbm = pl.BlockSpec(memory_space=pl.ANY)
    part = rows // ranks
    return pl.pallas_call(
        functools.partial(ladder_kernel, ranks, pairs),
        out_shape=jax.ShapeDtypeStruct((ranks, KT_DEV, rows // ranks, TILE), jnp.bfloat16),
        in_specs=[smem, smem, hbm, hbm],
        out_specs=vmem,
        scratch_shapes=[
            pltpu.VMEM((ranks, rows, width), jnp.bfloat16),
            pltpu.VMEM((tiles * pairs, TILE, width), jnp.bfloat16),
            pltpu.VMEM((KT_DEV, rows, width), jnp.bfloat16),
            pltpu.VMEM((rows, width), jnp.float32),
            pltpu.VMEM((ranks, KT_DEV, part, TILE), jnp.bfloat16),
            pltpu.VMEM((ranks * KT_DEV, part, TILE), jnp.bfloat16),
            pltpu.VMEM((ranks * KT_DEV, part, TILE), jnp.bfloat16),
            pltpu.VMEM((ranks, KT_DEV, part, TILE), jnp.bfloat16),
            pltpu.SemaphoreType.DMA((4,)),
            pltpu.SemaphoreType.DMA((4, ranks)),
            pltpu.SemaphoreType.DMA((ranks,)),
            pltpu.SemaphoreType.DMA((pairs - 1,)),
            pltpu.SemaphoreType.DMA((pairs - 1,)),
            pltpu.SemaphoreType.DMA((ranks - 1,)),
            pltpu.SemaphoreType.DMA((ranks - 1,)),
            pltpu.SemaphoreType.DMA((ranks - 1,)),
            pltpu.SemaphoreType.DMA((ranks - 1,)),
        ],
        compiler_params=pltpu.CompilerParams(
            collective_id=0, has_side_effects=True, vmem_limit_bytes=62 * 1024 * 1024
        ),
    )(tile_owner, screening, amplitudes, integrals.reshape(tiles, TILE, width))


def local(ranks, pairs, amplitudes, tile_owner, integrals, screening, occ_energy, virt_energy):
    pair_local = amplitudes.shape[0]
    tile_count = tile_owner.shape[0]
    width = KT_DEV * TILE
    column = lax.axis_index("vcol")
    owned_tiles = lax.dynamic_slice_in_dim(tile_owner, column * KT_DEV, KT_DEV, 0)
    back = ladder(ranks, pairs, amplitudes, tile_owner, integrals, screening)
    ladder_owned = back.transpose(0, 2, 1, 3).reshape(pair_local, width).astype(jnp.float32)
    virt_owned = jnp.dot(
        one_hot(owned_tiles, tile_count),
        virt_energy.reshape(tile_count, TILE),
        precision=lax.Precision.HIGHEST,
    ).reshape(width)
    residual = ladder_owned + (virt_owned[None, :] - occ_energy[:, None]) * amplitudes.astype(
        jnp.float32
    )
    return residual.astype(jnp.bfloat16)


def solution(mesh):
    return jax.shard_map(
        functools.partial(local, mesh.shape["vcol"], mesh.shape["pair"]),
        mesh=mesh,
        in_specs=(P("pair", "vcol"), P(), P("pair", "vcol"), P("pair", None, None), P("pair"), P()),
        out_specs=P("pair", "vcol"),
        check_vma=False,
    )
```

```python
import functools

import jax
import jax.numpy as jnp
from jax import lax
from jax.experimental import pallas as pl
from jax.experimental.pallas import tpu as pltpu
from jax.sharding import PartitionSpec as P

TILE = 128
PBLK = 64
KT_DEV = 2
MESH = pl.DeviceIdType.MESH


def one_hot(indices, length):
    return (indices[:, None] == jnp.arange(length, dtype=jnp.int32)[None, :]).astype(jnp.float32)


def ladder_kernel(
    ranks, pairs, owner, screen, amps, ints, out,
    gath, panel, lhs, acc, parts, natural, slots, landed,
    local_sem, send_sem, recv_sem, pair_send, pair_recv, out_send, out_recv, back_send, back_recv,
):
    length = ranks // 4
    me = lax.axis_index("vcol")
    core = lax.axis_index("pair")
    line, spot = me // 4, me % 4
    hi, lo = spot // 2, spot % 2
    turn = core % 2
    flip_lo, flip_hi = hi * 2 + 1 - lo, (1 - hi) * 2 + lo
    first = (1 - turn) * flip_lo + turn * flip_hi
    second = turn * flip_lo + (1 - turn) * flip_hi
    across = 3 - spot
    rows = gath.shape[1]
    blocks = rows // PBLK
    tiles = ints.shape[0]

    own_amps = pltpu.make_async_copy(amps, gath.at[me], local_sem.at[0])
    own_ints = pltpu.make_async_copy(ints, panel.at[pl.ds(core * tiles, tiles)], local_sem.at[1])
    own_amps.start()
    own_ints.start()

    has_up, has_down = line < length - 1, line > 0
    first_rank, second_rank = line * 4 + first, line * 4 + second
    barrier = pltpu.get_barrier_semaphore()

    def greet(target):
        pl.semaphore_signal(barrier, inc=1, device_id={"vcol": target}, device_id_type=MESH)

    def greet_step(step, _):
        greet((me + step) % ranks)
        return 0

    lax.fori_loop(1, ranks, greet_step, 0)
    for step in range(1, pairs):
        pl.semaphore_signal(
            barrier, inc=1, device_id={"pair": (core + step) % pairs}, device_id_type=MESH
        )

    pl.semaphore_wait(barrier, ranks - 1 + pairs - 1)

    cut = (blocks * 2 // 5) * PBLK
    bands = ((0, cut), (cut, rows))

    def shard(source, band, way, target):
        low, high = bands[band]
        place = gath.at[source, pl.ds(low, high - low)]
        return pltpu.make_async_remote_copy(
            src_ref=place, dst_ref=place,
            send_sem=send_sem.at[band, way, source], recv_sem=recv_sem.at[band, source],
            device_id={"vcol": target}, device_id_type=MESH,
        )

    def panel_copy(step):
        return pltpu.make_async_remote_copy(
            src_ref=ints, dst_ref=panel.at[pl.ds(core * tiles, tiles)],
            send_sem=pair_send.at[step - 1], recv_sem=pair_recv.at[step - 1],
            device_id={"pair": (core + step) % pairs}, device_id_type=MESH,
        )

    def arrived(source, band):
        shard(source, band, 3, second_rank).wait_recv()

    def multiply(source, band):
        low, high = bands[band]
        t0, t1 = owner[KT_DEV * source], owner[KT_DEV * source + 1]
        for slot, tile in enumerate((t0, t1)):
            columns = slice(slot * TILE, (slot + 1) * TILE)
            for block in range(low // PBLK, high // PBLK):
                part = slice(block * PBLK, (block + 1) * PBLK)
                value = gath[source, part, columns]
                for n in range(KT_DEV):
                    mark = screen[block, tile, KT_DEV * me + n].astype(jnp.float32)
                    lhs[n, part, columns] = value * jnp.full(value.shape, mark, jnp.float32).astype(
                        value.dtype
                    )
        right = jnp.concatenate([panel[t0], panel[t1]], axis=0)
        for n in range(KT_DEV):
            columns = slice(n * TILE, (n + 1) * TILE)
            acc[low:high, columns] += jnp.dot(
                lhs[n, low:high], right[:, columns], preferred_element_type=jnp.float32
            )

    def offset(e):
        return ((e + 1) // 2) * (1 - 2 * (e % 2))

    def inside(e):
        at = line + offset(e)
        return (at >= 0) & (at < length)

    own_amps.wait()

    def along_line(source, band, e, action):
        @pl.when(((e % 2 == 1) | (e == 0)) & has_up)
        def _():
            action(shard(source, band, 0, me + 4))

        @pl.when((e % 2 == 0) & has_down)
        def _():
            action(shard(source, band, 1, me - 4))

    def start(copy):
        copy.start()

    def wait_send(copy):
        copy.wait_send()

    def forward(source, band, e):
        along_line(source, band, e, start)
        shard(source, band, 2, first_rank).start()
        shard(source, band, 3, second_rank).start()

    for band in (1, 0):
        forward(me, band, jnp.int32(0))
    for step in range(1, pairs):
        panel_copy(step).start()
    acc[...] = jnp.zeros_like(acc)
    own_ints.wait()
    for step in range(1, pairs):
        panel_copy(step).wait_recv()
    for band in (1, 0):
        multiply(me, band)

    last = 2 * length - 1

    def on_column(e, _):
        source = (line + offset(e)) * 4 + spot

        @pl.when((e < last) & inside(e))
        def _():
            for band in (1, 0):
                arrived(source, band)
                forward(source, band, e)
            for band in (1, 0):
                multiply(source, band)

        late = e - 2
        beside = (line + offset(late)) * 4 + first

        @pl.when((late >= 0) & (late < last) & inside(late))
        def _():
            arrived(beside, 1)

            @pl.when(late == 0)
            def _():
                shard(beside, 1, 3, second_rank).start()

            arrived(beside, 0)
            shard(beside, 0, 3, second_rank).start()
            for band in (1, 0):
                multiply(beside, band)

        later = e - 4
        corner = (line + offset(later)) * 4 + across

        @pl.when((later >= 0) & inside(later))
        def _():
            arrived(corner, 1)
            along_line(corner, 1, later, start)
            multiply(corner, 1)

        return 0

    lax.fori_loop(1, last + 4, on_column, 0)

    def far_side(e, _):
        @pl.when((e < last) & inside(e))
        def _():
            source = (line + offset(e)) * 4 + second
            for band in (1, 0):
                arrived(source, band)
                multiply(source, band)

        late = e - 2

        @pl.when((late >= 0) & inside(late))
        def _():
            source = (line + offset(late)) * 4 + across
            arrived(source, 0)
            multiply(source, 0)

        return 0

    lax.fori_loop(0, last + 2, far_side, 0)

    part = rows // ranks
    for i in range(ranks):
        for n in range(KT_DEV):
            parts[i, n] = acc[i * part : (i + 1) * part, n * TILE : (n + 1) * TILE].astype(
                parts.dtype
            )

    def out_copy(step):
        target = (me + step) % ranks
        return pltpu.make_async_remote_copy(
            src_ref=parts.at[target], dst_ref=natural.at[pl.ds(KT_DEV * me, KT_DEV)],
            send_sem=out_send.at[step - 1], recv_sem=out_recv.at[step - 1],
            device_id={"vcol": target}, device_id_type=MESH,
        )

    def back_copy(step):
        target = (me + step) % ranks
        return pltpu.make_async_remote_copy(
            src_ref=slots.at[pl.ds(KT_DEV * target, KT_DEV)], dst_ref=landed.at[me],
            send_sem=back_send.at[step - 1], recv_sem=back_recv.at[step - 1],
            device_id={"vcol": target}, device_id_type=MESH,
        )

    def each_peer(action):
        def body(step, _):
            action(step)
            return 0

        lax.fori_loop(1, ranks, body, 0)

    own_out = pltpu.make_async_copy(
        parts.at[me], natural.at[pl.ds(KT_DEV * me, KT_DEV)], local_sem.at[2]
    )
    own_back = pltpu.make_async_copy(
        slots.at[pl.ds(KT_DEV * me, KT_DEV)], landed.at[me], local_sem.at[3]
    )
    each_peer(lambda step: out_copy(step).start())
    own_out.start()
    own_out.wait()
    each_peer(lambda step: out_copy(step).wait_recv())
    for slot in range(KT_DEV * ranks):
        slots[slot] = natural[owner[slot]]
    each_peer(lambda step: back_copy(step).start())
    own_back.start()
    own_back.wait()

    def drain(e, _):
        @pl.when(inside(e))
        def _():
            level = (line + offset(e)) * 4
            for band in (1, 0):
                along_line(level + spot, band, e, wait_send)
                shard(level + spot, band, 2, first_rank).wait_send()
                shard(level + spot, band, 3, second_rank).wait_send()
            shard(level + first, 0, 3, second_rank).wait_send()
            along_line(level + across, 1, e, wait_send)

        return 0

    shard(first_rank, 1, 3, second_rank).wait_send()
    lax.fori_loop(0, last, drain, 0)
    for step in range(1, pairs):
        panel_copy(step).wait_send()
    each_peer(lambda step: out_copy(step).wait_send())
    each_peer(lambda step: back_copy(step).wait_recv())
    out[...] = landed[...]
    each_peer(lambda step: back_copy(step).wait_send())


def ladder(ranks, pairs, amplitudes, tile_owner, integrals, screening):
    rows, width = amplitudes.shape
    tiles = integrals.shape[0] // TILE
    vmem, smem = pl.BlockSpec(memory_space=pltpu.VMEM), pl.BlockSpec(memory_space=pltpu.SMEM)
    hbm = pl.BlockSpec(memory_space=pl.ANY)
    part = rows // ranks
    return pl.pallas_call(
        functools.partial(ladder_kernel, ranks, pairs),
        out_shape=jax.ShapeDtypeStruct((ranks, KT_DEV, rows // ranks, TILE), jnp.bfloat16),
        in_specs=[smem, smem, hbm, hbm],
        out_specs=vmem,
        scratch_shapes=[
            pltpu.VMEM((ranks, rows, width), jnp.bfloat16),
            pltpu.VMEM((tiles * pairs, TILE, width), jnp.bfloat16),
            pltpu.VMEM((KT_DEV, rows, width), jnp.bfloat16),
            pltpu.VMEM((rows, width), jnp.float32),
            pltpu.VMEM((ranks, KT_DEV, part, TILE), jnp.bfloat16),
            pltpu.VMEM((ranks * KT_DEV, part, TILE), jnp.bfloat16),
            pltpu.VMEM((ranks * KT_DEV, part, TILE), jnp.bfloat16),
            pltpu.VMEM((ranks, KT_DEV, part, TILE), jnp.bfloat16),
            pltpu.SemaphoreType.DMA((4,)),
            pltpu.SemaphoreType.DMA((2, 4, ranks)),
            pltpu.SemaphoreType.DMA((2, ranks)),
            pltpu.SemaphoreType.DMA((pairs - 1,)),
            pltpu.SemaphoreType.DMA((pairs - 1,)),
            pltpu.SemaphoreType.DMA((ranks - 1,)),
            pltpu.SemaphoreType.DMA((ranks - 1,)),
            pltpu.SemaphoreType.DMA((ranks - 1,)),
            pltpu.SemaphoreType.DMA((ranks - 1,)),
        ],
        compiler_params=pltpu.CompilerParams(
            collective_id=0, has_side_effects=True, vmem_limit_bytes=62 * 1024 * 1024
        ),
    )(tile_owner, screening, amplitudes, integrals.reshape(tiles, TILE, width))


def local(ranks, pairs, amplitudes, tile_owner, integrals, screening, occ_energy, virt_energy):
    pair_local = amplitudes.shape[0]
    tile_count = tile_owner.shape[0]
    width = KT_DEV * TILE
    column = lax.axis_index("vcol")
    owned_tiles = lax.dynamic_slice_in_dim(tile_owner, column * KT_DEV, KT_DEV, 0)
    back = ladder(ranks, pairs, amplitudes, tile_owner, integrals, screening)
    ladder_owned = back.transpose(0, 2, 1, 3).reshape(pair_local, width).astype(jnp.float32)
    virt_owned = jnp.dot(
        one_hot(owned_tiles, tile_count),
        virt_energy.reshape(tile_count, TILE),
        precision=lax.Precision.HIGHEST,
    ).reshape(width)
    residual = ladder_owned + (virt_owned[None, :] - occ_energy[:, None]) * amplitudes.astype(
        jnp.float32
    )
    return residual.astype(jnp.bfloat16)


def solution(mesh):
    return jax.shard_map(
        functools.partial(local, mesh.shape["vcol"], mesh.shape["pair"]),
        mesh=mesh,
        in_specs=(P("pair", "vcol"), P(), P("pair", "vcol"), P("pair", None, None), P("pair"), P()),
        out_specs=P("pair", "vcol"),
        check_vma=False,
    )
```

```python
import functools

import jax
import jax.numpy as jnp
from jax import lax
from jax.experimental import pallas as pl
from jax.experimental.pallas import tpu as pltpu
from jax.sharding import PartitionSpec as P

TILE = 128
PBLK = 64
KT_DEV = 2
MESH = pl.DeviceIdType.MESH


def one_hot(indices, length):
    return (indices[:, None] == jnp.arange(length, dtype=jnp.int32)[None, :]).astype(jnp.float32)


def ladder_kernel(
    ranks, pairs, owner, screen, amps, ints, out,
    gath, panel, lhs, acc, parts, natural, slots, landed,
    local_sem, send_sem, recv_sem, pair_send, pair_recv, out_send, out_recv, back_send, back_recv,
):
    length = ranks // 4
    me = lax.axis_index("vcol")
    core = lax.axis_index("pair")
    line, spot = me // 4, me % 4
    hi, lo = spot // 2, spot % 2
    turn = core % 2
    flip_lo, flip_hi = hi * 2 + 1 - lo, (1 - hi) * 2 + lo
    first = (1 - turn) * flip_lo + turn * flip_hi
    second = turn * flip_lo + (1 - turn) * flip_hi
    across = 3 - spot
    rows = gath.shape[1]
    blocks = rows // PBLK
    tiles = ints.shape[0]

    own_amps = pltpu.make_async_copy(amps, gath.at[me], local_sem.at[0])
    own_ints = pltpu.make_async_copy(ints, panel.at[pl.ds(core * tiles, tiles)], local_sem.at[1])
    own_amps.start()
    own_ints.start()

    has_up, has_down = line < length - 1, line > 0
    first_rank, second_rank = line * 4 + first, line * 4 + second
    barrier = pltpu.get_barrier_semaphore()

    def greet(target):
        pl.semaphore_signal(barrier, inc=1, device_id={"vcol": target}, device_id_type=MESH)

    def greet_step(step, _):
        greet((me + step) % ranks)
        return 0

    lax.fori_loop(1, ranks, greet_step, 0)
    for step in range(1, pairs):
        pl.semaphore_signal(
            barrier, inc=1, device_id={"pair": (core + step) % pairs}, device_id_type=MESH
        )

    pl.semaphore_wait(barrier, ranks - 1 + pairs - 1)

    cut = (blocks * 3 // 5) * PBLK
    bands = ((0, cut), (cut, rows))

    def shard(source, band, way, target):
        low, high = bands[band]
        place = gath.at[source, pl.ds(low, high - low)]
        return pltpu.make_async_remote_copy(
            src_ref=place, dst_ref=place,
            send_sem=send_sem.at[band, way, source], recv_sem=recv_sem.at[band, source],
            device_id={"vcol": target}, device_id_type=MESH,
        )

    def panel_copy(step):
        return pltpu.make_async_remote_copy(
            src_ref=ints, dst_ref=panel.at[pl.ds(core * tiles, tiles)],
            send_sem=pair_send.at[step - 1], recv_sem=pair_recv.at[step - 1],
            device_id={"pair": (core + step) % pairs}, device_id_type=MESH,
        )

    def arrived(source, band):
        shard(source, band, 3, second_rank).wait_recv()

    def multiply(source, band):
        low, high = bands[band]
        t0, t1 = owner[KT_DEV * source], owner[KT_DEV * source + 1]
        for slot, tile in enumerate((t0, t1)):
            columns = slice(slot * TILE, (slot + 1) * TILE)
            for block in range(low // PBLK, high // PBLK):
                part = slice(block * PBLK, (block + 1) * PBLK)
                value = gath[source, part, columns]
                for n in range(KT_DEV):
                    mark = screen[block, tile, KT_DEV * me + n].astype(jnp.float32)
                    lhs[n, part, columns] = value * jnp.full(value.shape, mark, jnp.float32).astype(
                        value.dtype
                    )
        right = jnp.concatenate([panel[t0], panel[t1]], axis=0)
        for n in range(KT_DEV):
            columns = slice(n * TILE, (n + 1) * TILE)
            acc[low:high, columns] += jnp.dot(
                lhs[n, low:high], right[:, columns], preferred_element_type=jnp.float32
            )

    def offset(e):
        return ((e + 1) // 2) * (1 - 2 * (e % 2))

    def inside(e):
        at = line + offset(e)
        return (at >= 0) & (at < length)

    own_amps.wait()

    def along_line(source, band, e, action):
        @pl.when(((e % 2 == 1) | (e == 0)) & has_up)
        def _():
            action(shard(source, band, 0, me + 4))

        @pl.when((e % 2 == 0) & has_down)
        def _():
            action(shard(source, band, 1, me - 4))

    def start(copy):
        copy.start()

    def wait_send(copy):
        copy.wait_send()

    def forward(source, band, e):
        along_line(source, band, e, start)
        shard(source, band, 2, first_rank).start()
        shard(source, band, 3, second_rank).start()

    for band in (1, 0):
        forward(me, band, jnp.int32(0))
    for step in range(1, pairs):
        panel_copy(step).start()
    acc[...] = jnp.zeros_like(acc)
    own_ints.wait()
    for step in range(1, pairs):
        panel_copy(step).wait_recv()
    for band in (1, 0):
        multiply(me, band)

    last = 2 * length - 1

    def on_column(e, _):
        source = (line + offset(e)) * 4 + spot

        @pl.when((e < last) & inside(e))
        def _():
            for band in (1, 0):
                arrived(source, band)
                forward(source, band, e)
            for band in (1, 0):
                multiply(source, band)

        late = e - 2
        beside = (line + offset(late)) * 4 + first

        @pl.when((late >= 0) & (late < last) & inside(late))
        def _():
            arrived(beside, 1)

            @pl.when(late == 0)
            def _():
                shard(beside, 1, 3, second_rank).start()

            arrived(beside, 0)
            shard(beside, 0, 3, second_rank).start()
            for band in (1, 0):
                multiply(beside, band)

        later = e - 4
        corner = (line + offset(later)) * 4 + across

        @pl.when((later >= 0) & inside(later))
        def _():
            arrived(corner, 1)
            along_line(corner, 1, later, start)
            multiply(corner, 1)

        return 0

    lax.fori_loop(1, last + 4, on_column, 0)

    def far_side(e, _):
        @pl.when((e < last) & inside(e))
        def _():
            source = (line + offset(e)) * 4 + second
            for band in (1, 0):
                arrived(source, band)
                multiply(source, band)

        late = e - 2

        @pl.when((late >= 0) & inside(late))
        def _():
            source = (line + offset(late)) * 4 + across
            arrived(source, 0)
            multiply(source, 0)

        return 0

    lax.fori_loop(0, last + 2, far_side, 0)

    part = rows // ranks
    for i in range(ranks):
        for n in range(KT_DEV):
            parts[i, n] = acc[i * part : (i + 1) * part, n * TILE : (n + 1) * TILE].astype(
                parts.dtype
            )

    def out_copy(step):
        target = (me + step) % ranks
        return pltpu.make_async_remote_copy(
            src_ref=parts.at[target], dst_ref=natural.at[pl.ds(KT_DEV * me, KT_DEV)],
            send_sem=out_send.at[step - 1], recv_sem=out_recv.at[step - 1],
            device_id={"vcol": target}, device_id_type=MESH,
        )

    def back_copy(step):
        target = (me + step) % ranks
        return pltpu.make_async_remote_copy(
            src_ref=slots.at[pl.ds(KT_DEV * target, KT_DEV)], dst_ref=landed.at[me],
            send_sem=back_send.at[step - 1], recv_sem=back_recv.at[step - 1],
            device_id={"vcol": target}, device_id_type=MESH,
        )

    def each_peer(action):
        def body(step, _):
            action(step)
            return 0

        lax.fori_loop(1, ranks, body, 0)

    own_out = pltpu.make_async_copy(
        parts.at[me], natural.at[pl.ds(KT_DEV * me, KT_DEV)], local_sem.at[2]
    )
    own_back = pltpu.make_async_copy(
        slots.at[pl.ds(KT_DEV * me, KT_DEV)], landed.at[me], local_sem.at[3]
    )
    each_peer(lambda step: out_copy(step).start())
    own_out.start()
    own_out.wait()
    each_peer(lambda step: out_copy(step).wait_recv())
    for slot in range(KT_DEV * ranks):
        slots[slot] = natural[owner[slot]]
    each_peer(lambda step: back_copy(step).start())
    own_back.start()
    own_back.wait()

    def drain(e, _):
        @pl.when(inside(e))
        def _():
            level = (line + offset(e)) * 4
            for band in (1, 0):
                along_line(level + spot, band, e, wait_send)
                shard(level + spot, band, 2, first_rank).wait_send()
                shard(level + spot, band, 3, second_rank).wait_send()
            shard(level + first, 0, 3, second_rank).wait_send()
            along_line(level + across, 1, e, wait_send)

        return 0

    shard(first_rank, 1, 3, second_rank).wait_send()
    lax.fori_loop(0, last, drain, 0)
    for step in range(1, pairs):
        panel_copy(step).wait_send()
    each_peer(lambda step: out_copy(step).wait_send())
    each_peer(lambda step: back_copy(step).wait_recv())
    out[...] = landed[...]
    each_peer(lambda step: back_copy(step).wait_send())


def ladder(ranks, pairs, amplitudes, tile_owner, integrals, screening):
    rows, width = amplitudes.shape
    tiles = integrals.shape[0] // TILE
    vmem, smem = pl.BlockSpec(memory_space=pltpu.VMEM), pl.BlockSpec(memory_space=pltpu.SMEM)
    hbm = pl.BlockSpec(memory_space=pl.ANY)
    part = rows // ranks
    return pl.pallas_call(
        functools.partial(ladder_kernel, ranks, pairs),
        out_shape=jax.ShapeDtypeStruct((ranks, KT_DEV, rows // ranks, TILE), jnp.bfloat16),
        in_specs=[smem, smem, hbm, hbm],
        out_specs=vmem,
        scratch_shapes=[
            pltpu.VMEM((ranks, rows, width), jnp.bfloat16),
            pltpu.VMEM((tiles * pairs, TILE, width), jnp.bfloat16),
            pltpu.VMEM((KT_DEV, rows, width), jnp.bfloat16),
            pltpu.VMEM((rows, width), jnp.float32),
            pltpu.VMEM((ranks, KT_DEV, part, TILE), jnp.bfloat16),
            pltpu.VMEM((ranks * KT_DEV, part, TILE), jnp.bfloat16),
            pltpu.VMEM((ranks * KT_DEV, part, TILE), jnp.bfloat16),
            pltpu.VMEM((ranks, KT_DEV, part, TILE), jnp.bfloat16),
            pltpu.SemaphoreType.DMA((4,)),
            pltpu.SemaphoreType.DMA((2, 4, ranks)),
            pltpu.SemaphoreType.DMA((2, ranks)),
            pltpu.SemaphoreType.DMA((pairs - 1,)),
            pltpu.SemaphoreType.DMA((pairs - 1,)),
            pltpu.SemaphoreType.DMA((ranks - 1,)),
            pltpu.SemaphoreType.DMA((ranks - 1,)),
            pltpu.SemaphoreType.DMA((ranks - 1,)),
            pltpu.SemaphoreType.DMA((ranks - 1,)),
        ],
        compiler_params=pltpu.CompilerParams(
            collective_id=0, has_side_effects=True, vmem_limit_bytes=62 * 1024 * 1024
        ),
    )(tile_owner, screening, amplitudes, integrals.reshape(tiles, TILE, width))


def local(ranks, pairs, amplitudes, tile_owner, integrals, screening, occ_energy, virt_energy):
    pair_local = amplitudes.shape[0]
    tile_count = tile_owner.shape[0]
    width = KT_DEV * TILE
    column = lax.axis_index("vcol")
    owned_tiles = lax.dynamic_slice_in_dim(tile_owner, column * KT_DEV, KT_DEV, 0)
    back = ladder(ranks, pairs, amplitudes, tile_owner, integrals, screening)
    ladder_owned = back.transpose(0, 2, 1, 3).reshape(pair_local, width).astype(jnp.float32)
    virt_owned = jnp.dot(
        one_hot(owned_tiles, tile_count),
        virt_energy.reshape(tile_count, TILE),
        precision=lax.Precision.HIGHEST,
    ).reshape(width)
    residual = ladder_owned + (virt_owned[None, :] - occ_energy[:, None]) * amplitudes.astype(
        jnp.float32
    )
    return residual.astype(jnp.bfloat16)


def solution(mesh):
    return jax.shard_map(
        functools.partial(local, mesh.shape["vcol"], mesh.shape["pair"]),
        mesh=mesh,
        in_specs=(P("pair", "vcol"), P(), P("pair", "vcol"), P("pair", None, None), P("pair"), P()),
        out_specs=P("pair", "vcol"),
        check_vma=False,
    )
```

```python
import functools

import jax
import jax.numpy as jnp
from jax import lax
from jax.experimental import pallas as pl
from jax.experimental.pallas import tpu as pltpu
from jax.sharding import PartitionSpec as P

TILE = 128
PBLK = 64
KT_DEV = 2
MESH = pl.DeviceIdType.MESH


def one_hot(indices, length):
    return (indices[:, None] == jnp.arange(length, dtype=jnp.int32)[None, :]).astype(jnp.float32)


def ladder_kernel(
    ranks, pairs, owner, screen, amps, ints, out,
    gath, panel, lhs, acc, parts, natural, slots, landed,
    local_sem, send_sem, recv_sem, pair_send, pair_recv, out_send, out_recv, back_send, back_recv,
):
    length = ranks // 4
    me = lax.axis_index("vcol")
    core = lax.axis_index("pair")
    line, spot = me // 4, me % 4
    hi, lo = spot // 2, spot % 2
    turn = core % 2
    flip_lo, flip_hi = hi * 2 + 1 - lo, (1 - hi) * 2 + lo
    first = (1 - turn) * flip_lo + turn * flip_hi
    second = turn * flip_lo + (1 - turn) * flip_hi
    across = 3 - spot
    rows = gath.shape[1]
    blocks = rows // PBLK
    tiles = ints.shape[0]

    own_amps = pltpu.make_async_copy(amps, gath.at[me], local_sem.at[0])
    own_ints = pltpu.make_async_copy(ints, panel.at[pl.ds(core * tiles, tiles)], local_sem.at[1])
    own_amps.start()
    own_ints.start()

    has_up, has_down = line < length - 1, line > 0
    first_rank, second_rank = line * 4 + first, line * 4 + second
    barrier = pltpu.get_barrier_semaphore()

    def greet(target):
        pl.semaphore_signal(barrier, inc=1, device_id={"vcol": target}, device_id_type=MESH)

    def greet_step(step, _):
        greet((me + step) % ranks)
        return 0

    lax.fori_loop(1, ranks, greet_step, 0)
    for step in range(1, pairs):
        pl.semaphore_signal(
            barrier, inc=1, device_id={"pair": (core + step) % pairs}, device_id_type=MESH
        )

    pl.semaphore_wait(barrier, ranks - 1 + pairs - 1)

    cut = (blocks * 3 // 5) * PBLK
    bands = ((0, cut), (cut, rows))

    def shard(source, band, way, target):
        low, high = bands[band]
        place = gath.at[source, pl.ds(low, high - low)]
        return pltpu.make_async_remote_copy(
            src_ref=place, dst_ref=place,
            send_sem=send_sem.at[band, way, source], recv_sem=recv_sem.at[band, source],
            device_id={"vcol": target}, device_id_type=MESH,
        )

    def panel_copy(step):
        return pltpu.make_async_remote_copy(
            src_ref=ints, dst_ref=panel.at[pl.ds(core * tiles, tiles)],
            send_sem=pair_send.at[step - 1], recv_sem=pair_recv.at[step - 1],
            device_id={"pair": (core + step) % pairs}, device_id_type=MESH,
        )

    def arrived(source, band):
        shard(source, band, 3, second_rank).wait_recv()

    def multiply(source, band):
        low, high = bands[band]
        t0, t1 = owner[KT_DEV * source], owner[KT_DEV * source + 1]
        for slot, tile in enumerate((t0, t1)):
            columns = slice(slot * TILE, (slot + 1) * TILE)
            for block in range(low // PBLK, high // PBLK):
                part = slice(block * PBLK, (block + 1) * PBLK)
                value = gath[source, part, columns]
                for n in range(KT_DEV):
                    mark = screen[block, tile, KT_DEV * me + n].astype(jnp.float32)
                    lhs[n, part, columns] = value * jnp.full(value.shape, mark, jnp.float32).astype(
                        value.dtype
                    )
        right = jnp.concatenate([panel[t0], panel[t1]], axis=0)
        for n in range(KT_DEV):
            columns = slice(n * TILE, (n + 1) * TILE)
            acc[low:high, columns] += jnp.dot(
                lhs[n, low:high], right[:, columns], preferred_element_type=jnp.float32
            )

    def offset(e):
        return ((e + 1) // 2) * (1 - 2 * (e % 2))

    def inside(e):
        at = line + offset(e)
        return (at >= 0) & (at < length)

    own_amps.wait()

    def along_line(source, band, e, action):
        @pl.when(((e % 2 == 1) | (e == 0)) & has_up)
        def _():
            action(shard(source, band, 0, me + 4))

        @pl.when((e % 2 == 0) & has_down)
        def _():
            action(shard(source, band, 1, me - 4))

    def start(copy):
        copy.start()

    def wait_send(copy):
        copy.wait_send()

    def forward(source, band, e):
        along_line(source, band, e, start)
        shard(source, band, 2, first_rank).start()
        shard(source, band, 3, second_rank).start()

    for band in (1, 0):
        forward(me, band, jnp.int32(0))
    for step in range(1, pairs):
        panel_copy(step).start()
    acc[...] = jnp.zeros_like(acc)
    own_ints.wait()
    for step in range(1, pairs):
        panel_copy(step).wait_recv()
    for band in (1, 0):
        multiply(me, band)

    last = 2 * length - 1

    def on_column(e, _):
        source = (line + offset(e)) * 4 + spot

        @pl.when((e < last) & inside(e))
        def _():
            for band in (1, 0):
                arrived(source, band)
                forward(source, band, e)
            for band in (1, 0):
                multiply(source, band)

        late = e - 2
        beside = (line + offset(late)) * 4 + first

        @pl.when((late >= 0) & (late < last) & inside(late))
        def _():
            arrived(beside, 1)

            @pl.when(late == 0)
            def _():
                shard(beside, 1, 3, second_rank).start()

            arrived(beside, 0)
            shard(beside, 0, 3, second_rank).start()
            for band in (1, 0):
                multiply(beside, band)

        later = e - 4
        corner = (line + offset(later)) * 4 + across

        @pl.when((later >= 0) & inside(later))
        def _():
            arrived(corner, 1)
            along_line(corner, 1, later, start)
            multiply(corner, 1)

        return 0

    lax.fori_loop(1, last + 4, on_column, 0)

    def far_side(e, _):
        @pl.when((e < last) & inside(e))
        def _():
            source = (line + offset(e)) * 4 + second
            for band in (1, 0):
                arrived(source, band)
                multiply(source, band)

        late = e - 2

        @pl.when((late >= 0) & inside(late))
        def _():
            source = (line + offset(late)) * 4 + across
            arrived(source, 0)
            multiply(source, 0)

        return 0

    lax.fori_loop(0, last + 2, far_side, 0)

    part = rows // ranks
    for i in range(ranks):
        for n in range(KT_DEV):
            parts[i, n] = acc[i * part : (i + 1) * part, n * TILE : (n + 1) * TILE].astype(
                parts.dtype
            )

    def out_copy(step):
        target = (me + step) % ranks
        return pltpu.make_async_remote_copy(
            src_ref=parts.at[target], dst_ref=natural.at[pl.ds(KT_DEV * me, KT_DEV)],
            send_sem=out_send.at[step - 1], recv_sem=out_recv.at[step - 1],
            device_id={"vcol": target}, device_id_type=MESH,
        )

    def back_copy(step):
        target = (me + step) % ranks
        return pltpu.make_async_remote_copy(
            src_ref=slots.at[pl.ds(KT_DEV * target, KT_DEV)], dst_ref=landed.at[me],
            send_sem=back_send.at[step - 1], recv_sem=back_recv.at[step - 1],
            device_id={"vcol": target}, device_id_type=MESH,
        )

    def each_peer(action):
        def body(step, _):
            action(step)
            return 0

        lax.fori_loop(1, ranks, body, 0)

    own_out = pltpu.make_async_copy(
        parts.at[me], natural.at[pl.ds(KT_DEV * me, KT_DEV)], local_sem.at[2]
    )
    own_back = pltpu.make_async_copy(
        slots.at[pl.ds(KT_DEV * me, KT_DEV)], landed.at[me], local_sem.at[3]
    )
    each_peer(lambda step: out_copy(step).start())
    own_out.start()
    own_out.wait()
    each_peer(lambda step: out_copy(step).wait_recv())
    for slot in range(KT_DEV * ranks):
        slots[slot] = natural[owner[slot]]
    each_peer(lambda step: back_copy(step).start())
    own_back.start()
    own_back.wait()

    def drain(e, _):
        @pl.when(inside(e))
        def _():
            level = (line + offset(e)) * 4
            for band in (1, 0):
                along_line(level + spot, band, e, wait_send)
                shard(level + spot, band, 2, first_rank).wait_send()
                shard(level + spot, band, 3, second_rank).wait_send()
            shard(level + first, 0, 3, second_rank).wait_send()
            along_line(level + across, 1, e, wait_send)

        return 0

    shard(first_rank, 1, 3, second_rank).wait_send()
    lax.fori_loop(0, last, drain, 0)
    for step in range(1, pairs):
        panel_copy(step).wait_send()
    each_peer(lambda step: out_copy(step).wait_send())
    each_peer(lambda step: back_copy(step).wait_recv())
    for i in range(ranks):
        for n in range(KT_DEV):
            out[i * part : (i + 1) * part, n * TILE : (n + 1) * TILE] = landed[i, n].astype(out.dtype)
    each_peer(lambda step: back_copy(step).wait_send())


def ladder(ranks, pairs, amplitudes, tile_owner, integrals, screening):
    rows, width = amplitudes.shape
    tiles = integrals.shape[0] // TILE
    vmem, smem = pl.BlockSpec(memory_space=pltpu.VMEM), pl.BlockSpec(memory_space=pltpu.SMEM)
    hbm = pl.BlockSpec(memory_space=pl.ANY)
    part = rows // ranks
    return pl.pallas_call(
        functools.partial(ladder_kernel, ranks, pairs),
        out_shape=jax.ShapeDtypeStruct((rows, width), jnp.float32),
        in_specs=[smem, smem, hbm, hbm],
        out_specs=vmem,
        scratch_shapes=[
            pltpu.VMEM((ranks, rows, width), jnp.bfloat16),
            pltpu.VMEM((tiles * pairs, TILE, width), jnp.bfloat16),
            pltpu.VMEM((KT_DEV, rows, width), jnp.bfloat16),
            pltpu.VMEM((rows, width), jnp.float32),
            pltpu.VMEM((ranks, KT_DEV, part, TILE), jnp.bfloat16),
            pltpu.VMEM((ranks * KT_DEV, part, TILE), jnp.bfloat16),
            pltpu.VMEM((ranks * KT_DEV, part, TILE), jnp.bfloat16),
            pltpu.VMEM((ranks, KT_DEV, part, TILE), jnp.bfloat16),
            pltpu.SemaphoreType.DMA((4,)),
            pltpu.SemaphoreType.DMA((2, 4, ranks)),
            pltpu.SemaphoreType.DMA((2, ranks)),
            pltpu.SemaphoreType.DMA((pairs - 1,)),
            pltpu.SemaphoreType.DMA((pairs - 1,)),
            pltpu.SemaphoreType.DMA((ranks - 1,)),
            pltpu.SemaphoreType.DMA((ranks - 1,)),
            pltpu.SemaphoreType.DMA((ranks - 1,)),
            pltpu.SemaphoreType.DMA((ranks - 1,)),
        ],
        compiler_params=pltpu.CompilerParams(
            collective_id=0, has_side_effects=True, vmem_limit_bytes=62 * 1024 * 1024
        ),
    )(tile_owner, screening, amplitudes, integrals.reshape(tiles, TILE, width))


def local(ranks, pairs, amplitudes, tile_owner, integrals, screening, occ_energy, virt_energy):
    pair_local = amplitudes.shape[0]
    tile_count = tile_owner.shape[0]
    width = KT_DEV * TILE
    column = lax.axis_index("vcol")
    owned_tiles = lax.dynamic_slice_in_dim(tile_owner, column * KT_DEV, KT_DEV, 0)
    ladder_owned = ladder(ranks, pairs, amplitudes, tile_owner, integrals, screening)
    virt_owned = jnp.dot(
        one_hot(owned_tiles, tile_count),
        virt_energy.reshape(tile_count, TILE),
        precision=lax.Precision.HIGHEST,
    ).reshape(width)
    residual = ladder_owned + (virt_owned[None, :] - occ_energy[:, None]) * amplitudes.astype(
        jnp.float32
    )
    return residual.astype(jnp.bfloat16)


def solution(mesh):
    return jax.shard_map(
        functools.partial(local, mesh.shape["vcol"], mesh.shape["pair"]),
        mesh=mesh,
        in_specs=(P("pair", "vcol"), P(), P("pair", "vcol"), P("pair", None, None), P("pair"), P()),
        out_specs=P("pair", "vcol"),
        check_vma=False,
    )
```
